32 devices in a mesh: ckpt: 4 (over z), shard: 8 (over y, x, core).
Axes of the slice: x: 2, y: 2, z: 4, core: 2. Of those that a mesh axis runs over, the one named last changes fastest.
Arguments:
- task_vectors: bfloat16 [4, 4096, 16384], P('ckpt', 'shard'), may hold values from -0.125 to 0.125, as said below
- thresholds: float32 [4], replicated, may hold values from 0.009 to 0.062, as said below
- base_weight: float32 [4096, 16384], P('ckpt', 'shard'), may hold values from -0.3 to 0.3
Outputs:
- merged: float32 [4096, 16384], P('ckpt', 'shard')
The draws below stay inside these ranges and needn't reach their ends.
Inputs may be any that keep to these rules, and one draw needn't show every extreme that they name: `task_vectors`: every entry is a whole multiple of 2^-14. `thresholds`: every threshold is an odd multiple of 2^-15.
All inputs are finite; a program needn't handle non-finite values.
Results may differ from the reference program's by a relative error of at most 0.0003.
Values may be sent and summed in bfloat16 or wider, within the bound.
A program may use at most 128 MiB of HBM per device.

```python
import jax
import jax.numpy as jnp
from jax import lax

D = 4096
FFW = 16384
TASKS = 4


def draw_task_vectors(key, part):
    first_key, second_key = jax.random.split(key, 2)
    steps_count = jax.random.randint(first_key, (TASKS, D, FFW), -255, 256)
    exponent = jax.random.randint(second_key, (TASKS, D, FFW), 0, 4)
    values = steps_count.astype(jnp.float32) * jnp.exp2(exponent.astype(jnp.float32) - 14.0)
    return values.astype(jnp.bfloat16)


def draw_thresholds(key, part):
    middle = jax.random.randint(jax.random.fold_in(key, 11), (TASKS,), 160, 1000)
    return (2 * middle + 1).astype(jnp.float32) / 32768.0


def levels(key, dims, cuts, low, largest):
    level, own = 1.0, jax.random.fold_in(key, 6)
    for axis_at, blocks in cuts:
        draws = jnp.exp(jax.random.uniform(jax.random.fold_in(own, axis_at), (blocks,), jnp.float32, low / len(cuts), largest / len(cuts)))
        level = level * jnp.repeat(draws, dims[axis_at] // blocks).reshape([-1 if axis == axis_at else 1 for axis in range(len(dims))])
    return level


def normal_values(stream_key, extent, deviation, most, shards=(), kind=jnp.bfloat16):
    factor_of = levels(stream_key, extent, shards, -0.22, 0.18) if shards else 1.0
    values = jax.random.normal(stream_key, extent, jnp.float32) * deviation * factor_of
    return jnp.minimum(jnp.maximum(values, -most), most).astype(kind)


def setup_inputs(seed: int = 0) -> dict:
    splits = jax.random.split(jax.random.key(seed), 4)
    task_vectors = draw_task_vectors(jax.random.fold_in(splits[3], 71), 0)
    thresholds = draw_thresholds(jax.random.fold_in(splits[3], 71), 0)
    base_weight = normal_values(splits[2], (D, FFW), 0.05, 0.3, ((0, 4), (1, 8)), jnp.float32)
    return dict(task_vectors=task_vectors, thresholds=thresholds, base_weight=base_weight)


def trim_values(task_block, limit_value):
    values = task_block.astype(jnp.float32)
    return jnp.where(jnp.abs(values) > limit_value, values, jnp.float32(0.0))


def reference(task_vectors, thresholds, base_weight):
    def add_trimmed(running, inputs):
        return running + trim_values(inputs[0], inputs[1]), None

    zeros_block = jnp.zeros(base_weight.shape, jnp.float32)
    signed_total, unused = lax.scan(add_trimmed, zeros_block, (task_vectors, thresholds))

    def add_agreeing(running, inputs):
        trimmed = trim_values(inputs[0], inputs[1])
        agreeing = jnp.logical_or(jnp.logical_and(signed_total > 0, trimmed > 0),
                                  jnp.logical_and(signed_total < 0, trimmed < 0))
        kept_sum = running[0] + jnp.where(agreeing, trimmed, jnp.float32(0.0))
        agree_count = running[1] + agreeing.astype(jnp.float32)
        return (kept_sum, agree_count), None

    (kept_sum, agree_count), unused = lax.scan(add_agreeing, (zeros_block, zeros_block), (task_vectors, thresholds))
    disjoint = jnp.where(agree_count > 0, kept_sum / jnp.maximum(agree_count, 1.0), jnp.float32(0.0))
    return base_weight + disjoint
```

```python
import functools

import jax
import jax.numpy as jnp
from jax import lax
from jax.experimental import pallas as pl
from jax.experimental.pallas import tpu as pltpu
from jax.sharding import PartitionSpec as P

MESH = pl.DeviceIdType.MESH
CHUNK = 16
AHEAD = 3
LAG = 2


def merge_kernel(
    T, S, R, cw,
    thr_ref, x_ref, base_ref, out_ref,
    stage, recv, buf,
    s1_send, s1_recv, s2_send, s2_recv, own_sem, base_sem, out_sem,
):
    g = S // T
    RB, W = stage.shape[1], stage.shape[2]
    N = RB // R
    t = lax.axis_index("ckpt")
    s = lax.axis_index("shard")

    own = pltpu.make_async_copy(
        x_ref.at[0, :, pl.ds(pl.multiple_of(s * W, W), W)], stage.at[s], own_sem
    )
    base_in = pltpu.make_async_copy(base_ref, buf, base_sem)
    own.start()
    base_in.start()

    barrier = pltpu.get_barrier_semaphore()
    for d in range(1, S):
        pl.semaphore_signal(
            barrier, inc=1, device_id=(t, lax.rem(s + d, S)), device_id_type=MESH
        )
    for d in range(1, T):
        pl.semaphore_signal(
            barrier, inc=1, device_id=(lax.rem(t + d, T), s), device_id_type=MESH
        )
    pl.semaphore_wait(barrier, S - 1 + T - 1)

    def rows_of(j):
        return pl.ds(pl.multiple_of(j * R, R), R)

    def plane_copy(j, d):
        c = lax.rem(s + d, S)
        return pltpu.make_async_remote_copy(
            src_ref=x_ref.at[0, rows_of(j), pl.ds(pl.multiple_of(c * W, W), W)],
            dst_ref=stage.at[s, rows_of(j)],
            send_sem=s1_send.at[j],
            recv_sem=s1_recv.at[j],
            device_id=(t, c),
            device_id_type=MESH,
        )

    def line_copy(j, d):
        k = lax.rem(t + d, T)
        return pltpu.make_async_remote_copy(
            src_ref=stage.at[pl.ds(k * g, g), rows_of(j)],
            dst_ref=recv.at[T - d - 1, :, rows_of(j)],
            send_sem=s2_send.at[j],
            recv_sem=s2_recv.at[j],
            device_id=(k, s),
            device_id_type=MESH,
        )

    def plane_start(j):
        for d in range(S - 1, 0, -1):
            plane_copy(j, d).start()

    def plane_wait(sem, j):
        part = stage.at[pl.ds(0, S - 1), rows_of(j)]
        pltpu.make_async_copy(part, part, sem.at[j]).wait()

    def line_wait(sem, j):
        part = recv.at[:, :, rows_of(j)]
        pltpu.make_async_copy(part, part, sem.at[j]).wait()

    limits = [thr_ref[lax.rem(t + d, T)] for d in range(T)]

    def mean_rows(j):
        rows = rows_of(j)

        def cols_step(q, carry):
            cols = pl.ds(pl.multiple_of(q * cw, cw), cw)
            for i in range(g):
                trimmed = []
                for d in range(T):
                    if d == 0:
                        v = stage[t * g + i, rows, cols]
                    else:
                        v = recv[d - 1, i, rows, cols]
                    v = v.astype(jnp.float32)
                    trimmed.append(jnp.where(jnp.abs(v) > limits[d], v, 0.0))
                total = functools.reduce(jnp.add, trimmed)
                kept = jnp.zeros_like(total)
                count = jnp.zeros_like(total)
                for v in trimmed:
                    agree = v * total > 0
                    kept = kept + jnp.where(agree, v, 0.0)
                    count = count + jnp.where(agree, 1.0, 0.0)
                buf[i, rows, cols] = buf[i, rows, cols] + kept / jnp.maximum(count, 1.0)
            return carry

        lax.fori_loop(0, W // cw, cols_step, 0)

    def finish(j):
        line_wait(s2_recv, j)
        mean_rows(j)
        pltpu.make_async_copy(
            buf.at[:, rows_of(j)], out_ref.at[:, rows_of(j)], out_sem
        ).start()

    ahead = min(AHEAD, N)
    for j in range(ahead):
        plane_start(j)
    own.wait()
    base_in.wait()

    def step(j, carry):
        @pl.when(j + ahead < N)
        def _():
            plane_start(j + ahead)

        plane_wait(s1_recv, j)
        for d in range(T - 1, 0, -1):
            line_copy(j, d).start()

        @pl.when(j >= LAG)
        def _():
            finish(j - LAG)

        return carry

    lax.fori_loop(0, N, step, 0)

    def tail(j, carry):
        finish(j)
        return carry

    lax.fori_loop(N - LAG, N, tail, 0)

    def drain(j, carry):
        plane_wait(s1_send, j)
        line_wait(s2_send, j)
        return carry

    lax.fori_loop(0, N, drain, 0)
    pltpu.make_async_copy(buf, out_ref, out_sem).wait()


def local(task_vectors, thresholds, base_weight):
    T = lax.axis_size("ckpt")
    S = lax.axis_size("shard")
    RB = task_vectors.shape[1]
    W = task_vectors.shape[2] // S
    g = S // T
    R = min(CHUNK, RB)
    N = RB // R
    merged = pl.pallas_call(
        functools.partial(merge_kernel, T, S, R, min(W, 256)),
        out_shape=jax.ShapeDtypeStruct((g, RB, W), jnp.float32),
        in_specs=[
            pl.BlockSpec(memory_space=pltpu.SMEM),
            pl.BlockSpec(memory_space=pl.ANY),
            pl.BlockSpec(memory_space=pl.ANY),
        ],
        out_specs=pl.BlockSpec(memory_space=pl.ANY),
        scratch_shapes=[
            pltpu.VMEM((S, RB, W), jnp.bfloat16),
            pltpu.VMEM((T - 1, g, RB, W), jnp.bfloat16),
            pltpu.VMEM((g, RB, W), jnp.float32),
            pltpu.SemaphoreType.DMA((N,)),
            pltpu.SemaphoreType.DMA((N,)),
            pltpu.SemaphoreType.DMA((N,)),
            pltpu.SemaphoreType.DMA((N,)),
            pltpu.SemaphoreType.DMA,
            pltpu.SemaphoreType.DMA,
            pltpu.SemaphoreType.DMA,
        ],
        compiler_params=pltpu.CompilerParams(
            collective_id=0, has_side_effects=True, vmem_limit_bytes=60 * 1024 * 1024
        ),
        name="merge_exchange",
    )(thresholds, task_vectors, base_weight.reshape(g, RB, W))
    return merged.reshape(base_weight.shape)


def solution(mesh):
    placed = (P("ckpt", "shard", None), P(), P("ckpt", "shard"))
    return jax.shard_map(
        local, mesh=mesh, in_specs=placed, out_specs=P("ckpt", "shard"), check_vma=False
    )
```

```python
import functools

import jax
import jax.numpy as jnp
from jax import lax
from jax.experimental import pallas as pl
from jax.experimental.pallas import tpu as pltpu
from jax.sharding import PartitionSpec as P

MESH = pl.DeviceIdType.MESH
CHUNK = 16
AHEAD = 3
LAG = 2


def merge_kernel(
    T, S, R, cw,
    thr_ref, x_ref, base_ref, buf,
    stage, recv, thr,
    s1_send, s1_recv, s2_send, s2_recv, own_sem, base_sem, thr_sem,
):
    g = S // T
    RB, W = stage.shape[1], stage.shape[2]
    N = RB // R
    t = lax.axis_index("ckpt")
    s = lax.axis_index("shard")

    own = pltpu.make_async_copy(
        x_ref.at[0, :, pl.ds(pl.multiple_of(s * W, W), W)], stage.at[s], own_sem
    )
    base_in = pltpu.make_async_copy(base_ref, buf, base_sem)
    thr_in = pltpu.make_async_copy(thr_ref, thr, thr_sem)
    thr_in.start()
    own.start()
    base_in.start()

    barrier = pltpu.get_barrier_semaphore()
    for d in range(1, S):
        pl.semaphore_signal(
            barrier, inc=1, device_id=(t, lax.rem(s + d, S)), device_id_type=MESH
        )
    for d in range(1, T):
        pl.semaphore_signal(
            barrier, inc=1, device_id=(lax.rem(t + d, T), s), device_id_type=MESH
        )
    pl.semaphore_wait(barrier, S - 1 + T - 1)

    def rows_of(j):
        return pl.ds(pl.multiple_of(j * R, R), R)

    mine = lax.div(s, g)
    offsets = [0, T // 2] + [e for e in range(1, T) if e != T // 2]

    def plane_copy(j, e, q):
        c = lax.rem(mine + e, T) * g + lax.rem(lax.rem(s, g) + q, g)
        return pltpu.make_async_remote_copy(
            src_ref=x_ref.at[0, rows_of(j), pl.ds(pl.multiple_of(c * W, W), W)],
            dst_ref=stage.at[s, rows_of(j)],
            send_sem=s1_send.at[j],
            recv_sem=s1_recv.at[j, mine],
            device_id=(t, c),
            device_id_type=MESH,
        )

    def line_copy(j, k):
        return pltpu.make_async_remote_copy(
            src_ref=stage.at[pl.ds(k * g, g), rows_of(j)],
            dst_ref=recv.at[lax.rem(t - k - 1 + T, T), :, rows_of(j)],
            send_sem=s2_send.at[j],
            recv_sem=s2_recv.at[j],
            device_id=(k, s),
            device_id_type=MESH,
        )

    def plane_start(j):
        for e in offsets[1:] + offsets[:1]:
            for q in range(g):
                if e or q:
                    plane_copy(j, e, q).start()

    def plane_arrived(j, e):
        count = g if e else g - 1
        if count:
            part = stage.at[pl.ds(0, count), rows_of(j)]
            sem = s1_recv.at[j, lax.rem(mine + e, T)]
            pltpu.make_async_copy(part, part, sem).wait()

    def plane_sent(j):
        part = stage.at[pl.ds(0, S - 1), rows_of(j)]
        pltpu.make_async_copy(part, part, s1_send.at[j]).wait()

    def line_wait(sem, j):
        part = recv.at[:, :, rows_of(j)]
        pltpu.make_async_copy(part, part, sem.at[j]).wait()

    def mean_rows(j):
        limits = [thr[lax.rem(t + d, T)] for d in range(T)]
        rows = rows_of(j)

        def cols_step(q, carry):
            cols = pl.ds(pl.multiple_of(q * cw, cw), cw)
            for i in range(g):
                trimmed = []
                for d in range(T):
                    if d == 0:
                        v = stage[t * g + i, rows, cols]
                    else:
                        v = recv[d - 1, i, rows, cols]
                    v = v.astype(jnp.float32)
                    trimmed.append(jnp.where(jnp.abs(v) > limits[d], v, 0.0))
                total = functools.reduce(jnp.add, trimmed)
                kept = jnp.zeros_like(total)
                count = jnp.zeros_like(total)
                for v in trimmed:
                    agree = v * total > 0
                    kept = kept + jnp.where(agree, v, 0.0)
                    count = count + jnp.where(agree, 1.0, 0.0)
                buf[i, rows, cols] = buf[i, rows, cols] + kept / jnp.maximum(count, 1.0)
            return carry

        lax.fori_loop(0, W // cw, cols_step, 0)

    def finish(j):
        line_wait(s2_recv, j)
        mean_rows(j)

    ahead = min(AHEAD, N)
    for j in range(ahead):
        plane_start(j)
    own.wait()
    base_in.wait()
    thr_in.wait()

    def step(j, carry):
        @pl.when(j + ahead < N)
        def _():
            plane_start(j + ahead)

        for e in offsets:
            k = lax.rem(mine + e, T)
            plane_arrived(j, e)

            @pl.when(k != t)
            def _():
                line_copy(j, k).start()

        @pl.when(j >= LAG)
        def _():
            finish(j - LAG)

        return carry

    lax.fori_loop(0, N, step, 0)

    def tail(j, carry):
        finish(j)
        return carry

    lax.fori_loop(N - LAG, N, tail, 0)

    def drain(j, carry):
        plane_sent(j)
        line_wait(s2_send, j)
        return carry

    lax.fori_loop(0, N, drain, 0)


def local(task_vectors, thresholds, base_weight):
    T = lax.axis_size("ckpt")
    S = lax.axis_size("shard")
    RB = task_vectors.shape[1]
    W = task_vectors.shape[2] // S
    g = S // T
    R = min(CHUNK, RB)
    N = RB // R
    merged = pl.pallas_call(
        functools.partial(merge_kernel, T, S, R, min(W, 256)),
        out_shape=pltpu.VMEM((g, RB, W), jnp.float32),
        in_specs=[
            pl.BlockSpec(memory_space=pltpu.HBM),
            pl.BlockSpec(memory_space=pltpu.HBM),
            pl.BlockSpec(memory_space=pltpu.HBM),
        ],
        out_specs=pl.BlockSpec(memory_space=pltpu.VMEM),
        scratch_shapes=[
            pltpu.VMEM((S, RB, W), jnp.bfloat16),
            pltpu.VMEM((T - 1, g, RB, W), jnp.bfloat16),
            pltpu.SMEM((T,), jnp.float32),
            pltpu.SemaphoreType.DMA((N,)),
            pltpu.SemaphoreType.DMA((N, T)),
            pltpu.SemaphoreType.DMA((N,)),
            pltpu.SemaphoreType.DMA((N,)),
            pltpu.SemaphoreType.DMA,
            pltpu.SemaphoreType.DMA,
            pltpu.SemaphoreType.DMA,
        ],
        compiler_params=pltpu.CompilerParams(
            collective_id=0, has_side_effects=True, vmem_limit_bytes=40 * 1024 * 1024
        ),
        name="merge_exchange",
    )(thresholds, task_vectors, base_weight.reshape(g, RB, W))
    return merged.reshape(base_weight.shape)


def solution(mesh):
    placed = (P("ckpt", "shard", None), P(), P("ckpt", "shard"))
    return jax.shard_map(
        local, mesh=mesh, in_specs=placed, out_specs=P("ckpt", "shard"), check_vma=False
    )
```

```python
import functools

import jax
import jax.numpy as jnp
from jax import lax
from jax.experimental import pallas as pl
from jax.experimental.pallas import tpu as pltpu
from jax.sharding import PartitionSpec as P

MESH = pl.DeviceIdType.MESH
VMEM_BYTES = 67043328
CHUNK = 16
AHEAD = 3
LAG = 4


def merge_kernel(
    T, S, R, cw,
    thr_ref, x_ref, base_ref, buf,
    stage, recv, thr,
    s1_send, s1_recv, s2_send, s2_recv, own_sem, base_sem, thr_sem,
):
    g = S // T
    RB, W = stage.shape[1], stage.shape[2]
    N = RB // R
    t = lax.axis_index("ckpt")
    s = lax.axis_index("shard")

    own = pltpu.make_async_copy(
        x_ref.at[0, :, pl.ds(pl.multiple_of(s * W, W), W)], stage.at[s], own_sem
    )
    base_in = pltpu.make_async_copy(base_ref, buf, base_sem)
    thr_in = pltpu.make_async_copy(thr_ref, thr, thr_sem)
    thr_in.start()
    own.start()
    base_in.start()

    barrier = pltpu.get_barrier_semaphore()
    for d in range(1, S):
        pl.semaphore_signal(
            barrier, inc=1, device_id=(t, lax.rem(s + d, S)), device_id_type=MESH
        )
    for d in range(1, T):
        pl.semaphore_signal(
            barrier, inc=1, device_id=(lax.rem(t + d, T), s), device_id_type=MESH
        )
    pl.semaphore_wait(barrier, S - 1 + T - 1)

    def rows_of(j):
        return pl.ds(pl.multiple_of(j * R, R), R)

    mine = lax.div(s, g)
    sign = 2 * lax.rem(mine, 2) - 1
    offsets = [(0, 0)]
    if T > 1:
        offsets.append((1, T // 2))
    for i in range(1, (T + 1) // 2):
        offsets += [(1, T - sign * i), (1, T + sign * i)]

    def plane_copy(j, e, q):
        c = lax.rem(mine + e[1], T) * g + lax.rem(lax.rem(s, g) + q, g)
        return pltpu.make_async_remote_copy(
            src_ref=x_ref.at[0, rows_of(j), pl.ds(pl.multiple_of(c * W, W), W)],
            dst_ref=stage.at[s, rows_of(j)],
            send_sem=s1_send.at[j],
            recv_sem=s1_recv.at[j, mine],
            device_id=(t, c),
            device_id_type=MESH,
        )

    def line_copy(j, k):
        return pltpu.make_async_remote_copy(
            src_ref=stage.at[pl.ds(k * g, g), rows_of(j)],
            dst_ref=recv.at[lax.rem(t - k - 1 + T, T), :, rows_of(j)],
            send_sem=s2_send.at[j],
            recv_sem=s2_recv.at[j],
            device_id=(k, s),
            device_id_type=MESH,
        )

    def plane_start(j):
        for e in offsets[1:] + offsets[:1]:
            for q in range(g):
                if e[0] or q:
                    plane_copy(j, e, q).start()

    def plane_arrived(j, e):
        count = g if e[0] else g - 1
        if count:
            part = stage.at[pl.ds(0, count), rows_of(j)]
            sem = s1_recv.at[j, lax.rem(mine + e[1], T)]
            pltpu.make_async_copy(part, part, sem).wait()

    def plane_sent(j):
        part = stage.at[pl.ds(0, S - 1), rows_of(j)]
        pltpu.make_async_copy(part, part, s1_send.at[j]).wait()

    def line_wait(sem, j):
        part = recv.at[:, :, rows_of(j)]
        pltpu.make_async_copy(part, part, sem.at[j]).wait()

    def mean_rows(j):
        limits = [thr[lax.rem(t + d, T)] for d in range(T)]
        rows = rows_of(j)

        def cols_step(q, carry):
            cols = pl.ds(pl.multiple_of(q * cw, cw), cw)
            for i in range(g):
                trimmed = []
                for d in range(T):
                    if d == 0:
                        v = stage[t * g + i, rows, cols]
                    else:
                        v = recv[d - 1, i, rows, cols]
                    v = v.astype(jnp.float32)
                    trimmed.append(jnp.where(jnp.abs(v) > limits[d], v, 0.0))
                total = functools.reduce(jnp.add, trimmed)
                kept = jnp.zeros_like(total)
                count = jnp.zeros_like(total)
                for v in trimmed:
                    agree = v * total > 0
                    kept = kept + jnp.where(agree, v, 0.0)
                    count = count + jnp.where(agree, 1.0, 0.0)
                buf[i, rows, cols] = buf[i, rows, cols] + kept / jnp.maximum(count, 1.0)
            return carry

        lax.fori_loop(0, W // cw, cols_step, 0)

    def finish(j):
        line_wait(s2_recv, j)
        mean_rows(j)

    ahead = min(AHEAD, N)
    for j in range(ahead):
        plane_start(j)
    own.wait()
    base_in.wait()
    thr_in.wait()

    def step(j, carry):
        @pl.when(j + ahead < N)
        def _():
            plane_start(j + ahead)

        for e in offsets:
            k = lax.rem(mine + e[1], T)
            plane_arrived(j, e)

            @pl.when(k != t)
            def _():
                line_copy(j, k).start()

        @pl.when(j >= LAG)
        def _():
            finish(j - LAG)

        return carry

    lax.fori_loop(0, N, step, 0)

    def tail(j, carry):
        finish(j)
        return carry

    lax.fori_loop(N - LAG, N, tail, 0)

    def drain(j, carry):
        plane_sent(j)
        line_wait(s2_send, j)
        return carry

    lax.fori_loop(0, N, drain, 0)


def local(task_vectors, thresholds, base_weight):
    T = lax.axis_size("ckpt")
    S = lax.axis_size("shard")
    RB = task_vectors.shape[1]
    W = task_vectors.shape[2] // S
    g = S // T
    R = min(CHUNK, RB)
    N = RB // R
    merged = pl.pallas_call(
        functools.partial(merge_kernel, T, S, R, min(W, 256)),
        out_shape=pltpu.VMEM((g, RB, W), jnp.float32),
        in_specs=[
            pl.BlockSpec(memory_space=pltpu.HBM),
            pl.BlockSpec(memory_space=pltpu.HBM),
            pl.BlockSpec(memory_space=pltpu.HBM),
        ],
        out_specs=pl.BlockSpec(memory_space=pltpu.VMEM),
        scratch_shapes=[
            pltpu.VMEM((S, RB, W), jnp.bfloat16),
            pltpu.VMEM((T - 1, g, RB, W), jnp.bfloat16),
            pltpu.SMEM((T,), jnp.float32),
            pltpu.SemaphoreType.DMA((N,)),
            pltpu.SemaphoreType.DMA((N, T)),
            pltpu.SemaphoreType.DMA((N,)),
            pltpu.SemaphoreType.DMA((N,)),
            pltpu.SemaphoreType.DMA,
            pltpu.SemaphoreType.DMA,
            pltpu.SemaphoreType.DMA,
        ],
        compiler_params=pltpu.CompilerParams(
            collective_id=0, has_side_effects=True, vmem_limit_bytes=VMEM_BYTES - g * RB * W * 4
        ),
        name="merge_exchange",
    )(thresholds, task_vectors, base_weight.reshape(g, RB, W))
    return merged.reshape(base_weight.shape)


def solution(mesh):
    placed = (P("ckpt", "shard", None), P(), P("ckpt", "shard"))
    return jax.shard_map(
        local, mesh=mesh, in_specs=placed, out_specs=P("ckpt", "shard"), check_vma=False
    )
```
